128 devices in a mesh: row: 8 (over x, core), col: 16 (over z, y).
Axes of the slice: x: 4, y: 4, z: 4, core: 2. Of those that a mesh axis runs over, the one named last changes fastest.
Arguments:
- attention: bfloat16 [4096, 5120], P('row', 'col'), may hold values from -6 to 6
- attention_tan: bfloat16 [4096, 5120], P('row', 'col'), may hold values from -6 to 6
- residual: bfloat16 [4096, 5120], P('row', 'col'), may hold values from -6 to 6
- residual_tan: bfloat16 [4096, 5120], P('row', 'col'), may hold values from -6 to 6
- modulation: float32 [4, 5120], replicated, may hold values from -3 to 3
- modulation_tan: float32 [4, 5120], replicated, may hold values from -3 to 3
- w_out: bfloat16 [5120, 5120], P('row', 'col'), may hold values from -0.078125 to 0.078125
- b_out: float32 [5120], P('col'), may hold values from -3 to 3
- w_up: bfloat16 [5120, 13824], P('row', 'col'), may hold values from -0.078125 to 0.078125
- b_up: float32 [13824], P('col'), may hold values from -3 to 3
- w_down: bfloat16 [13824, 5120], P('col', 'row'), may hold values from -0.0625 to 0.0625
- b_down: float32 [5120], P('col'), may hold values from -3 to 3
Outputs:
- block_out: bfloat16 [4096, 5120], P('row', 'col')
- block_tan: bfloat16 [4096, 5120], P('row', 'col')
The draws below stay inside these ranges and needn't reach their ends.
All inputs are finite; a program needn't handle non-finite values.
Results may differ from the reference program's by a relative error of at most 0.011.
Values may be sent and summed in bfloat16 or wider, within the bound.
No kernel may reach another device: no remote copies, remote signals or barrier semaphores. Data moves between devices by JAX's collectives and lax.ppermute only.
A program may use at most 128 MiB of HBM per device.

```python
import math
import jax
import jax.numpy as jnp
from jax import lax

D = 5120
FF = 13824
TOKENS = 4096
N_COL = 16


def spiked(drawn, key, source, target, blocks, factor):
    owner, partner = [(jnp.arange(drawn.shape[axis_at]) // (drawn.shape[axis_at] // blocks)).reshape([-1 if axis == axis_at else 1 for axis in range(drawn.ndim)]) for axis_at in (source, target)]
    chosen = jax.random.permutation(key, blocks)[partner]
    strong = (owner == chosen) | (owner == (partner + blocks // 2) % blocks)
    return jnp.where(strong, factor * drawn, drawn)


def steps_of(stream_key, extent, cuts, least, high):
    factor_of = 1.0
    for position, parts in cuts:
        draws = jax.random.uniform(jax.random.fold_in(jax.random.fold_in(stream_key, 6), position), (parts,), jnp.float32, least / len(cuts), high / len(cuts))
        factor_of = factor_of * jnp.repeat(jnp.exp(draws), extent[position] // parts).reshape((-1,) + (1,) * (len(extent) - 1 - position))
    return factor_of


def noise(rng, dims, spread, most, cuts=(), dtype=jnp.bfloat16):
    entries = jax.random.normal(rng, dims, jnp.float32) * spread
    if len(cuts) > 0:
        entries = steps_of(rng, dims, cuts, -0.22, 0.18) * entries
    return jnp.clip(entries, min=-most, max=most).astype(dtype)


def noise_with(own_key, extent, scale, bound, split, heavy, kind=jnp.bfloat16):
    array = scale * jax.random.normal(own_key, extent, jnp.float32)
    if split:
        array = array * steps_of(own_key, extent, split, -0.22, 0.18)
    return jnp.clip(spiked(array, jax.random.fold_in(own_key, 3), *heavy), -bound, bound).astype(kind)


def setup_inputs(seed: int = 0) -> dict:
    key_list = jax.random.split(jax.random.key(seed), 13)
    return {
        "attention": noise(key_list[0], (TOKENS, D), 1.0, 6.0, ((0, 8), (1, 16))),
        "attention_tan": noise(key_list[1], (TOKENS, D), 1.0, 6.0, ((0, 8), (1, 16))),
        "residual": noise(key_list[2], (TOKENS, D), 1.0, 6.0, ((0, 8), (1, 16))),
        "residual_tan": noise(key_list[3], (TOKENS, D), 1.0, 6.0, ((0, 8), (1, 16))),
        "modulation": noise(key_list[4], (4, D), 0.5, 3.0, (), jnp.float32),
        "modulation_tan": noise(key_list[5], (4, D), 0.5, 3.0, (), jnp.float32),
        "w_out": noise(key_list[6], (D, D), D ** -0.5, 0.078125, ((0, 8), (1, 16))),
        "b_out": noise(key_list[7], (D,), 0.5, 3.0, ((0, 16),), jnp.float32),
        "w_up": noise(key_list[8], (D, FF), D ** -0.5, 0.078125, ((0, 8), (1, 16))),
        "b_up": noise(key_list[9], (FF,), 0.5, 3.0, ((0, 16),), jnp.float32),
        "w_down": noise_with(key_list[10], (FF, D), FF ** -0.5, 0.0625, ((0, 16), (1, 8)), (0, 1, 16, 2.0)),
        "b_down": noise(key_list[11], (D,), 0.5, 3.0, ((0, 16),), jnp.float32),
    }


def gelu_pair(values, tangent):
    coeff = math.sqrt(2.0 / math.pi)
    inner = coeff * (values + 0.044715 * values * values * values)
    tanh_value = jnp.tanh(inner)
    primal = 0.5 * values * (1.0 + tanh_value)
    slope = 0.5 * (1.0 + tanh_value) + 0.5 * values * (1.0 - tanh_value * tanh_value) * coeff * (1.0 + 3.0 * 0.044715 * values * values)
    return (primal, slope * tangent)

def block_sums(activ, w_down):
    count = activ.shape[0]
    block = FF // N_COL
    pieces = activ.reshape(count, N_COL, block).transpose(1, 0, 2)
    weights = w_down.reshape(N_COL, block, D)

    def step(carry, pair):
        part = jnp.dot(pair[0], pair[1], preferred_element_type=jnp.float32).astype(jnp.bfloat16)
        return (carry + part.astype(jnp.float32), None)
    total, unused = lax.scan(step, jnp.zeros((count, D), jnp.float32), (pieces, weights))
    return total

def reference(attention, attention_tan, residual, residual_tan, modulation, modulation_tan, w_out, b_out, w_up, b_up, w_down, b_down):
    projected = jnp.dot(attention, w_out, preferred_element_type=jnp.float32) + b_out
    projected_tan = jnp.dot(attention_tan, w_out, preferred_element_type=jnp.float32)
    stream = (residual.astype(jnp.float32) + modulation[0] * projected).astype(jnp.bfloat16)
    stream_tan = (residual_tan.astype(jnp.float32) + modulation_tan[0] * projected + modulation[0] * projected_tan).astype(jnp.bfloat16)
    values = stream.astype(jnp.float32)
    values_tan = stream_tan.astype(jnp.float32)
    count = values.shape[1]
    mean = lax.optimization_barrier(jnp.sum(values, axis=1, keepdims=True)) / count
    square = lax.optimization_barrier(jnp.sum(values * values, axis=1, keepdims=True)) / count
    mean_tan = lax.optimization_barrier(jnp.sum(values_tan, axis=1, keepdims=True)) / count
    cross = lax.optimization_barrier(jnp.sum(values * values_tan, axis=1, keepdims=True)) / count
    recip = jax.lax.rsqrt(square - mean * mean + 1e-06)
    normed = (values - mean) * recip
    normed_tan = recip * (values_tan - mean_tan) - normed * recip * recip * (cross - mean * mean_tan)
    inputs = (normed * (1.0 + modulation[2]) + modulation[1]).astype(jnp.bfloat16)
    inputs_tan = (normed_tan * (1.0 + modulation[2]) + normed * modulation_tan[2] + modulation_tan[1]).astype(jnp.bfloat16)
    hidden_pre = jnp.dot(inputs, w_up, preferred_element_type=jnp.float32) + b_up
    hidden_tan = jnp.dot(inputs_tan, w_up, preferred_element_type=jnp.float32)
    activ, activ_tan = gelu_pair(hidden_pre, hidden_tan)
    activ = activ.astype(jnp.bfloat16)
    activ_tan = activ_tan.astype(jnp.bfloat16)
    feed = block_sums(activ, w_down) + b_down
    feed_tan = block_sums(activ_tan, w_down)
    block_out = (values + modulation[3] * feed).astype(jnp.bfloat16)
    block_tan = (values_tan + modulation_tan[3] * feed + modulation[3] * feed_tan).astype(jnp.bfloat16)
    return (block_out, block_tan)
```

```python
import functools
import math

import jax
import jax.numpy as jnp
from jax import lax
from jax.experimental import pallas as pl
from jax.experimental.pallas import tpu as pltpu
from jax.sharding import PartitionSpec as P


BF16 = jnp.bfloat16
F32 = jnp.float32
SHIFTS = (0, 1, 3, 2)
CHUNKS = 2
GELU_C = math.sqrt(2.0 / math.pi)


def chip_of(index):
    row, col = divmod(index, 16)
    x, core = divmod(row, 2)
    z, y = divmod(col, 4)
    return x, core, z, y


def index_of(x, core, z, y):
    return (x * 2 + core) * 16 + z * 4 + y


def torus_perm(phase, shift):
    pairs = []
    for index in range(128):
        x, core, z, y = chip_of(index)
        if core == phase:
            y = (y + shift) % 4
        else:
            z = (z + shift) % 4
        pairs.append((index, index_of(x, core, z, y)))
    return pairs


def x_perm(shift):
    pairs = []
    for index in range(128):
        x, core, z, y = chip_of(index)
        pairs.append((index, index_of((x + shift) % 4, core, z, y)))
    return pairs


def core_perm():
    return [(i, index_of(c[0], 1 - c[1], c[2], c[3])) for i, c in ((i, chip_of(i)) for i in range(128))]


BOTH = ("row", "col")


def send(value, phase, shift):
    return lax.ppermute(value, BOTH, torus_perm(phase, shift))


def send_x(value, shift):
    return lax.ppermute(value, BOTH, x_perm(shift))


def gather_block(block):
    near = [send(block, 0, 1), send(block, 0, -1), send(block, 0, 2)]
    group = jnp.concatenate([block] + near, axis=0)
    half = group.shape[0] // 2
    plus = send(group, 1, 1)
    minus = send(group, 1, -1)
    far = [send(plus[:half], 1, 1), send(minus[half:], 1, -1)]
    return [block] + near + [plus, minus] + far


def gather_weight(block):
    half = block.shape[0] // 2
    plus = send_x(block, 1)
    minus = send_x(block, -1)
    ring = [block, plus, minus, send_x(plus[:half], 1), send_x(minus[half:], -1)]
    return ring + [lax.ppermute(piece, BOTH, core_perm()) for piece in ring]


def token_copies(pieces, index_ref, dest, sem, rows):
    copies = []

    def add(source, slot):
        start = pl.multiple_of(index_ref[slot] * rows, rows)
        copies.append(pltpu.make_async_copy(source, dest.at[pl.ds(start, rows), :], sem.at[slot]))

    for slot in range(4):
        add(pieces[slot], slot)
    for group, ref in ((1, pieces[4]), (2, pieces[5])):
        for slot in range(4):
            add(ref.at[pl.ds(slot * rows, rows), :], group * 4 + slot)
    for slot in range(4):
        ref = pieces[6 + slot // 2]
        add(ref.at[pl.ds((slot % 2) * rows, rows), :], 12 + slot)
    return copies


def weight_parts(pieces):
    parts = []
    for side in range(2):
        own = pieces[side * 5 : side * 5 + 5]
        full = own[0].shape[0]
        half = full // 2
        parts += [(own[0], 0, full, side * 4), (own[1], 0, full, side * 4 + 1), (own[2], 0, full, side * 4 + 2)]
        parts += [(own[3], 0, half, side * 4 + 3), (own[4], half, half, side * 4 + 3)]
    return parts


def weight_copies(pieces, index_ref, dest, sem, along_rows):
    copies = []
    for number, (ref, first, count, slot) in enumerate(weight_parts(pieces)):
        row = index_ref[32 + slot]
        if along_rows:
            start = pl.multiple_of(row * pieces[0].shape[0] + first, 16)
            target = dest.at[pl.ds(start, count), :]
        else:
            width = pieces[0].shape[1]
            target = dest.at[pl.ds(first, count), pl.ds(pl.multiple_of(row * width, width), width)]
        copies.append(pltpu.make_async_copy(ref, target, sem.at[number]))
    return copies


def project_kernel(index_ref, cols_ref, res_ref, *refs):
    tokens, weights = refs[:8], refs[8:18]
    out_ref, values, matrix, acc, sem_t, sem_w = refs[18:]
    rows = res_ref.shape[0]
    copies = weight_copies(weights, index_ref, matrix, sem_w, False)
    copies += token_copies(tokens, index_ref, values, sem_t, rows)
    for copy in copies:
        copy.start()
    for copy in copies:
        copy.wait()
    depth = values.shape[0]
    step = 1280
    half = res_ref.shape[1] // 2
    for k in range(0, depth, step):
        part = jnp.dot(matrix[:, k : k + step], values[k : k + step, :], preferred_element_type=F32)
        if k == 0:
            acc[...] = part
        else:
            acc[...] += part
    gate, gate_tan, bias = cols_ref[:, 0:1], cols_ref[:, 1:2], cols_ref[:, 2:3]
    primal = acc[:, :half] + bias
    out_ref[:, :half] = (res_ref[:, :half].astype(F32) + gate * primal).astype(BF16)
    out_ref[:, half:] = (res_ref[:, half:].astype(F32) + gate_tan * primal + gate * acc[:, half:]).astype(BF16)


def up_kernel(index_ref, mods_ref, bias_ref, *refs):
    tokens, weights = refs[:8], refs[8:18]
    out_ref, values, matrix, acc, sem_t, sem_w = refs[18:]
    rows = tokens[0].shape[0]
    half = values.shape[1] // 2
    depth = values.shape[0]
    t_copies = token_copies(tokens, index_ref, values, sem_t, rows)
    w_copies = weight_copies(weights, index_ref, matrix, sem_w, False)
    for copy in t_copies + w_copies:
        copy.start()
    for copy in t_copies:
        copy.wait()
    block = 64

    def sums(i, carry):
        rows_i = pl.ds(pl.multiple_of(i * block, block), block)
        p = values[rows_i, :half].astype(F32)
        t = values[rows_i, half:].astype(F32)

        def fold(v):
            return jnp.sum(v.reshape(block // 8, 8, half), axis=0)

        return (carry[0] + fold(p), carry[1] + fold(p * p), carry[2] + fold(t), carry[3] + fold(p * t))

    zero = jnp.zeros((8, half), F32)
    totals = lax.fori_loop(0, depth // block, sums, (zero, zero, zero, zero))
    mean, square, mean_tan, cross = (jnp.sum(v, axis=0, keepdims=True) / depth for v in totals)
    recip = lax.rsqrt(square - mean * mean + 1e-06)
    slope = recip * recip * (cross - mean * mean_tan)

    def norm(i, carry):
        rows_i = pl.ds(pl.multiple_of(i * block, block), block)
        p = values[rows_i, :half].astype(F32)
        t = values[rows_i, half:].astype(F32)
        shift, scale = mods_ref[rows_i, 0:1], mods_ref[rows_i, 1:2]
        shift_tan, scale_tan = mods_ref[rows_i, 2:3], mods_ref[rows_i, 3:4]
        normed = (p - mean) * recip
        normed_tan = recip * (t - mean_tan) - normed * slope
        values[rows_i, :half] = (normed * scale + shift).astype(BF16)
        values[rows_i, half:] = (normed_tan * scale + normed * scale_tan + shift_tan).astype(BF16)
        return carry

    lax.fori_loop(0, depth // block, norm, 0)
    for copy in w_copies:
        copy.wait()
    step = 1280
    for k in range(0, depth, step):
        part = jnp.dot(matrix[:, k : k + step], values[k : k + step, :], preferred_element_type=F32)
        if k == 0:
            acc[...] = part
        else:
            acc[...] += part
    tile = 96

    def gelu(i, carry):
        rows_i = pl.ds(pl.multiple_of(i * tile, tile), tile)
        v = acc[rows_i, :half] + bias_ref[rows_i, 0:1]
        tangent = acc[rows_i, half:]
        tanh_value = jnp.tanh(GELU_C * (v + 0.044715 * v * v * v))
        out_ref[rows_i, :half] = (0.5 * v * (1.0 + tanh_value)).astype(BF16)
        slope_v = 0.5 * (1.0 + tanh_value) + 0.5 * v * (1.0 - tanh_value * tanh_value) * GELU_C * (
            1.0 + 3.0 * 0.044715 * v * v
        )
        out_ref[rows_i, half:] = (slope_v * tangent).astype(BF16)
        return carry

    lax.fori_loop(0, acc.shape[0] // tile, gelu, 0)


def down_kernel(index_ref, act_ref, *refs):
    weights = refs[:10]
    outs = refs[10:17]
    matrix, stage, sem_w, sem_o = refs[17:]
    rows = stage.shape[1]
    copies = weight_copies(weights, index_ref, matrix, sem_w, True)
    for copy in copies:
        copy.start()
    for copy in copies:
        copy.wait()
    order = [(2, 0), (2, 1), (2, 2), (2, 3), (1, 0), (1, 1), (1, 2), (1, 3), (3, 0), (3, 1), (3, 2), (3, 3)]
    order += [(0, 0), (0, 1), (0, 2), (0, 3)]
    pending = []
    for number, (j, i) in enumerate(order):
        start = pl.multiple_of(index_ref[16 + j * 4 + i] * rows, rows)
        stage[number] = jnp.dot(
            matrix[pl.ds(start, rows), :], act_ref[...], preferred_element_type=F32
        ).astype(BF16)
        if j == 0:
            target = outs[6].at[pl.ds(i * rows, rows), :]
        else:
            target = outs[(2, 1, 3).index(j) * 2 + i // 2].at[pl.ds((i % 2) * rows, rows), :]
        copy = pltpu.make_async_copy(stage.at[number], target, sem_o.at[number])
        copy.start()
        pending.append(copy)
    for copy in pending:
        copy.wait()


SMEM = pl.BlockSpec(memory_space=pltpu.SMEM)
VMEM = pl.BlockSpec(memory_space=pltpu.VMEM)
ANY = pl.BlockSpec(memory_space=pl.ANY)


def cost(m, k, n, extra):
    return pl.CostEstimate(flops=2 * m * k * n, bytes_accessed=2 * (m * k + k * n) + extra, transcendentals=0)


def project(index, cols, residual, tokens, weights):
    rows, width = residual.shape
    depth = rows * 16
    return pl.pallas_call(
        project_kernel,
        out_shape=jax.ShapeDtypeStruct((rows, width), BF16),
        in_specs=[SMEM, VMEM, VMEM] + [ANY] * 18,
        out_specs=VMEM,
        scratch_shapes=[
            pltpu.VMEM((depth, width), BF16),
            pltpu.VMEM((rows, depth), BF16),
            pltpu.VMEM((rows, width), F32),
            pltpu.SemaphoreType.DMA((16,)),
            pltpu.SemaphoreType.DMA((10,)),
        ],
        cost_estimate=cost(rows, depth, width, 0),
        name="project",
    )(index, cols, residual, *tokens, *weights)


def up(index, mods, bias, tokens, weights):
    rows, width = tokens[0].shape
    depth = rows * 16
    hidden = weights[0].shape[0]
    return pl.pallas_call(
        up_kernel,
        out_shape=jax.ShapeDtypeStruct((hidden, width), BF16),
        in_specs=[SMEM, VMEM, VMEM] + [ANY] * 18,
        out_specs=VMEM,
        scratch_shapes=[
            pltpu.VMEM((depth, width), BF16),
            pltpu.VMEM((hidden, depth), BF16),
            pltpu.VMEM((hidden, width), F32),
            pltpu.SemaphoreType.DMA((16,)),
            pltpu.SemaphoreType.DMA((10,)),
        ],
        cost_estimate=cost(hidden, depth, width, 0),
        name="up",
    )(index, mods, bias, *tokens, *weights)


def down(index, act, weights):
    hidden, width = act.shape
    rows = weights[0].shape[0] // 2
    depth = rows * 16
    pair = jax.ShapeDtypeStruct((2 * rows, width), BF16)
    return pl.pallas_call(
        down_kernel,
        out_shape=[pair] * 6 + [jax.ShapeDtypeStruct((4 * rows, width), BF16)],
        in_specs=[SMEM, VMEM] + [ANY] * 10,
        out_specs=[ANY] * 7,
        scratch_shapes=[
            pltpu.VMEM((depth, hidden), BF16),
            pltpu.VMEM((16, rows, width), BF16),
            pltpu.SemaphoreType.DMA((10,)),
            pltpu.SemaphoreType.DMA((16,)),
        ],
        cost_estimate=cost(depth, hidden, width, 2 * depth * width),
        name="down",
    )(index, act, *weights)


def add(*values):
    total = values[0].astype(F32)
    for value in values[1:]:
        total = total + value.astype(F32)
    return total


def scatter_sum(parts):
    far_a, far_b, plus_a, plus_b, minus_a, minus_b, own = parts
    half = far_a.shape[0]
    rows = half // 2
    from_far_a = send(far_a, 1, 1)
    from_far_b = send(far_b, 1, -1)
    got_plus_b = send(plus_b, 1, 1)
    got_minus_a = send(minus_a, 1, -1)
    got_plus_a = send(add(plus_a, from_far_a).astype(BF16), 1, 1)
    got_minus_b = send(add(minus_b, from_far_b).astype(BF16), 1, -1)
    low = add(own[:half], got_plus_a, got_minus_a)
    high = add(own[half:], got_plus_b, got_minus_b)
    near = [
        send(low[rows:].astype(BF16), 0, 1),
        send(high[rows:].astype(BF16), 0, -1),
        send(high[:rows].astype(BF16), 0, 2),
    ]
    return add(low[:rows], *near)


def index_table():
    row, col = lax.axis_index("row"), lax.axis_index("col")
    x, core = row // 2, row % 2
    z, y = col // 4, col % 4
    first, second = jnp.where(core == 0, y, z), jnp.where(core == 0, z, y)

    def column(one, two):
        return jnp.where(core == 0, two % 4 * 4 + one % 4, one % 4 * 4 + two % 4)

    shifts = jnp.array(SHIFTS, jnp.int32)
    plain = jnp.arange(4, dtype=jnp.int32)
    sources = column((first - shifts + 4)[None, :], (second - shifts + 4)[:, None]).reshape(16)
    targets = column((first + plain)[None, :], (second + plain)[:, None]).reshape(16)
    ring = (x - shifts + 4) % 4 * 2
    return jnp.concatenate([sources, targets, ring + core, ring + 1 - core]).astype(jnp.int32)


def body(
    attention,
    attention_tan,
    residual,
    residual_tan,
    modulation,
    modulation_tan,
    w_out,
    b_out,
    w_up,
    b_up,
    w_down,
    b_down,
):
    width = residual.shape[1]
    tokens = residual.shape[0] // CHUNKS
    index = index_table()
    col_offset = lax.axis_index("col") * width
    local = lax.dynamic_slice_in_dim(modulation, col_offset, width, 1)
    local_tan = lax.dynamic_slice_in_dim(modulation_tan, col_offset, width, 1)
    zero = jnp.zeros_like(b_out)
    cols = jnp.stack([local[0], local_tan[0], b_out, local[3], local_tan[3], b_down, zero, zero], axis=1)
    ones = jnp.zeros_like(modulation[1])
    mods = jnp.stack([modulation[1], 1.0 + modulation[2], modulation_tan[1], modulation_tan[2]] + [ones] * 4, axis=1)
    up_bias = jnp.broadcast_to(b_up[:, None], (b_up.shape[0], 8))

    def chunk(primal, tangent, c):
        part = slice(c * tokens, (c + 1) * tokens)
        return jnp.concatenate([primal.T[:, part], tangent.T[:, part]], axis=1)

    weights_out = gather_weight(w_out.T)
    weights_up = gather_weight(w_up.T)
    weights_down = gather_weight(w_down.T)
    streams, acts = [], []
    for c in range(CHUNKS):
        gathered = gather_block(chunk(attention, attention_tan, c))
        streams.append(project(index, cols, chunk(residual, residual_tan, c), gathered, weights_out))
    outs = []
    for c in range(CHUNKS):
        act = up(index, mods, up_bias, gather_block(streams[c]), weights_up)
        feeds = scatter_sum(down(index, act, weights_down))
        feed = feeds[:, :tokens] + cols[:, 5:6]
        feed_tan = feeds[:, tokens:]
        stream = streams[c].astype(F32)
        gate, gate_tan = cols[:, 3:4], cols[:, 4:5]
        out = (stream[:, :tokens] + gate * feed).astype(BF16)
        out_tan = (stream[:, tokens:] + gate_tan * feed + gate * feed_tan).astype(BF16)
        outs.append((out, out_tan))
    return tuple(jnp.concatenate([o[k] for o in outs], axis=1).T for k in range(2))


def solution(mesh):
    placed = (
        P("row", "col"),
        P("row", "col"),
        P("row", "col"),
        P("row", "col"),
        P(),
        P(),
        P("row", "col"),
        P("col"),
        P("row", "col"),
        P("col"),
        P("col", "row"),
        P("col"),
    )
    return jax.shard_map(
        body,
        mesh=mesh,
        in_specs=placed,
        out_specs=(P("row", "col"), P("row", "col")),
        check_vma=False,
    )
```

```python
import functools
import math

import jax
import jax.numpy as jnp
from jax import lax
from jax.experimental import pallas as pl
from jax.experimental.pallas import tpu as pltpu
from jax.sharding import PartitionSpec as P


BF16 = jnp.bfloat16
F32 = jnp.float32
SHIFTS = (0, 1, 3, 2)
CHUNKS = 2
GELU_C = math.sqrt(2.0 / math.pi)


def chip_of(index):
    row, col = divmod(index, 16)
    x, core = divmod(row, 2)
    z, y = divmod(col, 4)
    return x, core, z, y


def index_of(x, core, z, y):
    return (x * 2 + core) * 16 + z * 4 + y


def torus_perm(phase, shift):
    pairs = []
    for index in range(128):
        x, core, z, y = chip_of(index)
        if core == phase:
            y = (y + shift) % 4
        else:
            z = (z + shift) % 4
        pairs.append((index, index_of(x, core, z, y)))
    return pairs


def x_perm(shift):
    pairs = []
    for index in range(128):
        x, core, z, y = chip_of(index)
        pairs.append((index, index_of((x + shift) % 4, core, z, y)))
    return pairs


def core_perm():
    return [(i, index_of(c[0], 1 - c[1], c[2], c[3])) for i, c in ((i, chip_of(i)) for i in range(128))]


BOTH = ("row", "col")


def send(value, phase, shift):
    return lax.ppermute(value, BOTH, torus_perm(phase, shift))


def send_x(value, shift):
    return lax.ppermute(value, BOTH, x_perm(shift))


def partner(value):
    return lax.ppermute(value, BOTH, core_perm())


def gather_block(block, extra=()):
    near = [send(block, 0, 1), send(block, 0, -1), send(block, 0, 2)]
    group = jnp.concatenate([block] + near, axis=0)
    if extra:
        group, *extra = lax.optimization_barrier((group, *extra))
    half = group.shape[0] // 2
    plus = send(group, 1, 1)
    minus = send(group, 1, -1)
    far = [send(plus[:half], 1, 1), send(minus[half:], 1, -1)]
    pieces = [block] + near + [plus, minus] + far
    return (pieces, extra) if extra else pieces


def gather_weight(block, direct):
    plus = send_x(block, 1)
    minus = send_x(block, -1)
    ring = [block, plus, minus]
    if direct:
        ring.append(send_x(block, 2))
    else:
        half = block.shape[0] // 2
        ring += [send_x(plus[:half], 1), send_x(minus[half:], -1)]
    return ring + [partner(piece) for piece in ring]


def token_copies(pieces, index_ref, dest, sem, rows):
    copies = []
    places = [(n, 0) for n in range(4)] + [(n, k) for n in (4, 5) for k in range(4)]
    places += [(n, k) for n in (6, 7) for k in range(2)]
    for slot, (piece, k) in enumerate(places):
        column = index_ref[slot]
        target = dest.at[pl.ds(pl.multiple_of(column * rows, rows), rows), :]
        copies.append(pltpu.make_async_copy(pieces[piece].at[pl.ds(k * rows, rows), :], target, sem.at[column]))
    return copies


def wait_tokens(column, source, dest, sem, rows):
    target = dest.at[pl.ds(pl.multiple_of(column * rows, rows), rows), :]
    pltpu.make_async_copy(source, target, sem.at[column]).wait()


def weight_parts(pieces):
    parts = []
    count = len(pieces) // 2
    for side in range(2):
        own = pieces[side * count : side * count + count]
        full = own[0].shape[0]
        parts += [(own[n], 0, full, side * 4 + n) for n in range(3)]
        for n in range(3, count):
            size = own[n].shape[0]
            parts.append((own[n], (n - 3) * size, size, side * 4 + 3))
    return parts


def weight_copies(pieces, index_ref, dest, sem, along_rows, by_slot):
    copies = []
    for ref, first, count, slot in weight_parts(pieces):
        place = slot if by_slot else index_ref[32 + slot]
        if along_rows:
            start = place * pieces[0].shape[0] + first
            target = dest.at[pl.ds(start if by_slot else pl.multiple_of(start, 16), count), :]
        else:
            width = pieces[0].shape[1]
            start = place * width
            target = dest.at[pl.ds(first, count), pl.ds(start if by_slot else pl.multiple_of(start, width), width)]
        copies.append(pltpu.make_async_copy(ref, target, sem.at[place]))
    return copies


def project_kernel(count, c, index_ref, cols_ref, res_ref, res_tan_ref, *refs):
    tokens, weights = refs[:8], refs[8 : 8 + count]
    out_ref, values, matrix, acc, sem_t, sem_w = refs[8 + count :]
    rows, width = acc.shape
    half = width // 2
    here = slice(c * half, c * half + half)
    for copy in token_copies(tokens, index_ref, values, sem_t, rows):
        copy.start()
    for copy in weight_copies(weights, index_ref, matrix, sem_w, False, False):
        copy.start()
    step = 2 * rows
    acc[...] = jnp.zeros_like(acc)

    def block(k, carry):
        wait_tokens(2 * k, tokens[0], values, sem_t, rows)
        wait_tokens(2 * k + 1, tokens[0], values, sem_t, rows)
        depth = pl.ds(pl.multiple_of(k * step, step), step)
        pltpu.make_async_copy(weights[0], matrix.at[:, depth], sem_w.at[k]).wait()
        acc[...] += jnp.dot(matrix[:, depth], values[depth, :], preferred_element_type=F32)
        return carry

    lax.fori_loop(0, 8, block, 0)
    gate, gate_tan, bias = cols_ref[:, 0:1], cols_ref[:, 1:2], cols_ref[:, 2:3]
    primal = acc[:, :half] + bias
    out_ref[:, :half] = (res_ref[:, here].astype(F32) + gate * primal).astype(BF16)
    out_ref[:, half:] = (res_tan_ref[:, here].astype(F32) + gate_tan * primal + gate * acc[:, half:]).astype(BF16)


def widen_kernel(mods_ref, select_ref, out_ref):
    def widen(i, carry):
        part = pl.ds(pl.multiple_of(i * 256, 256), 256)
        out_ref[part, :] = lax.dot_general(
            mods_ref[:, part], select_ref[...], (((0,), (0,)), ((), ())), preferred_element_type=F32
        )
        return carry

    lax.fori_loop(0, out_ref.shape[0] // 256, widen, 0)


def up_kernel(count_up, index_ref, spread, bias_ref, *refs):
    tokens, refs = refs[:8], refs[8:]
    up, refs = refs[:count_up], refs[count_up:]
    act, values, normed, w_up, acc, sem_t, sem_u = refs
    rows = tokens[0].shape[0]
    depth, width = values.shape
    half = width // 2
    step = 2 * rows
    for copy in token_copies(tokens, index_ref, values, sem_t, rows):
        copy.start()


    for copy in weight_copies(up, index_ref, w_up, sem_u, False, True):
        copy.start()

    def fold(v):
        return jnp.sum(v.reshape(v.shape[0] // 8, 8, half), axis=0)

    def column_sums(column, carry):
        wait_tokens(column, tokens[0], values, sem_t, rows)

        def sums(i, carry):
            part = pl.ds(pl.multiple_of(column * rows + i * 64, 64), 64)
            p = values[part, :half].astype(F32)
            t = values[part, half:].astype(F32)
            return (carry[0] + fold(p), carry[1] + fold(p * p), carry[2] + fold(t), carry[3] + fold(p * t))

        return lax.fori_loop(0, rows // 64, sums, carry)

    zero = jnp.zeros((8, half), F32)
    totals = lax.fori_loop(0, 16, column_sums, (zero,) * 4)
    mean, square, mean_tan, cross = (jnp.sum(v, axis=0, keepdims=True) / depth for v in totals)
    recip = lax.rsqrt(square - mean * mean + 1e-06)
    slope = recip * recip * (cross - mean * mean_tan)

    def norm(slot, start, first, size):
        source = pl.ds(start, size)
        target = pl.ds(first, size)
        for lane in range(0, half, 128):
            here = slice(lane, lane + 128)
            there = slice(half + lane, half + lane + 128)
            p = values[source, here].astype(F32)
            t = values[source, there].astype(F32)
            shift, scale, shift_tan, scale_tan = (spread[source, n * 128 : n * 128 + 128] for n in range(4))
            unit = (p - mean[:, here]) * recip[:, here]
            unit_tan = recip[:, here] * (t - mean_tan[:, here]) - unit * slope[:, here]
            normed[slot, target, here] = (unit * scale + shift).astype(BF16)
            normed[slot, target, there] = (unit_tan * scale + unit * scale_tan + shift_tan).astype(BF16)

    def norm_first(i, carry):
        start = pl.multiple_of(i * 64, 64)
        norm(0, pl.multiple_of(index_ref[32] * step + start, 64), start, 64)
        return carry

    lax.fori_loop(0, step // 64, norm_first, 0)
    acc[...] = jnp.zeros_like(acc)

    def up_block(k, slot):
        lanes = pl.ds(pl.multiple_of(k * step, step), step)
        norm(1 - slot, pl.multiple_of(index_ref[32 + jnp.minimum(k + 1, 7)] * step, step), 0, step)
        acc[...] += jnp.dot(w_up[:, lanes], normed[slot], preferred_element_type=F32)

    def up_pair(i, carry):
        up_block(2 * i, 0)
        up_block(2 * i + 1, 1)
        return carry

    def up_group(g, carry):
        for n in range(4):
            row = g * 4 + n
            lanes = pl.ds(pl.multiple_of(row * step, step), step)
            pltpu.make_async_copy(up[0], w_up.at[:, lanes], sem_u.at[row]).wait()
        return lax.fori_loop(g * 2, g * 2 + 2, up_pair, carry)

    lax.fori_loop(0, 2, up_group, 0)
    tile = 96

    def gelu(i, carry):
        part = pl.ds(pl.multiple_of(i * tile, tile), tile)
        v = acc[part, :half] + bias_ref[part, 0:1]
        tangent = acc[part, half:]
        tanh_value = jnp.tanh(GELU_C * (v + 0.044715 * v * v * v))
        act[part, :half] = (0.5 * v * (1.0 + tanh_value)).astype(BF16)
        slope_v = 0.5 * (1.0 + tanh_value) + 0.5 * v * (1.0 - tanh_value * tanh_value) * GELU_C * (
            1.0 + 3.0 * 0.044715 * v * v
        )
        act[part, half:] = (slope_v * tangent).astype(BF16)
        return carry

    lax.fori_loop(0, acc.shape[0] // tile, gelu, 0)
    hidden = acc.shape[0]
    act[hidden:, :] = jnp.zeros((act.shape[0] - hidden, width), BF16)


def down_kernel(count, index_ref, act_ref, *refs):
    weights, outs = refs[:count], refs[count : count + 5]
    matrix, stage, sem_w, sem_o = refs[count + 5 :]
    step = weights[0].shape[0]
    rows = step // 2
    for copy in weight_copies(weights, index_ref, matrix, sem_w, True, True):
        copy.start()

    def block(r, carry):
        part = pl.ds(pl.multiple_of(r * step, step), step)
        pltpu.make_async_copy(weights[0], matrix.at[part, :], sem_w.at[r]).wait()
        place = pl.ds(pl.multiple_of(index_ref[32 + r] * step, step), step)
        stage[place, :] = jnp.dot(matrix[part, :], act_ref[...], preferred_element_type=F32).astype(BF16)
        return carry

    lax.fori_loop(0, 8, block, 0)
    copies = []
    for number, out in enumerate(outs):
        j = (2, 2, 1, 3, 0)[number]
        low = 2 if number == 1 else 0
        for i in range(out.shape[0] // rows):
            start = pl.multiple_of(index_ref[16 + j * 4 + low + i] * rows, rows)
            target = out.at[pl.ds(i * rows, rows), :]
            copies.append(pltpu.make_async_copy(stage.at[pl.ds(start, rows), :], target, sem_o.at[len(copies)]))
            copies[-1].start()
    for copy in copies:
        copy.wait()


def turn_kernel(in_ref, out_ref):
    rows = in_ref.shape[0]
    out_ref[:, rows:] = jnp.zeros((out_ref.shape[0], out_ref.shape[1] - rows), out_ref.dtype)
    for lane in range(0, in_ref.shape[1], 128):
        out_ref[lane : lane + 128, :rows] = in_ref[:, lane : lane + 128].T


SMEM = pl.BlockSpec(memory_space=pltpu.SMEM)
VMEM = pl.BlockSpec(memory_space=pltpu.VMEM)
ANY = pl.BlockSpec(memory_space=pl.ANY)


def turn(block):
    rows, columns = block.shape
    return pl.pallas_call(
        turn_kernel,
        out_shape=jax.ShapeDtypeStruct((columns, -(-rows // 128) * 128), block.dtype),
        in_specs=[VMEM],
        out_specs=VMEM,
    )(block)


def cost(flops, size):
    return pl.CostEstimate(flops=flops, bytes_accessed=size, transcendentals=0)


def project(c, index, cols, residual, residual_tan, tokens, weights):
    rows, width = tokens[0].shape
    depth = rows * 16
    return pl.pallas_call(
        functools.partial(project_kernel, len(weights), c),
        out_shape=jax.ShapeDtypeStruct((rows, width), BF16),
        in_specs=[SMEM, VMEM, VMEM, VMEM] + [ANY] * (8 + len(weights)),
        out_specs=VMEM,
        scratch_shapes=[
            pltpu.VMEM((depth, width), BF16),
            pltpu.VMEM((rows, depth), BF16),
            pltpu.VMEM((rows, width), F32),
            pltpu.SemaphoreType.DMA((16,)),
            pltpu.SemaphoreType.DMA((8,)),
        ],
        cost_estimate=cost(2 * rows * depth * width, 2 * depth * (rows + width)),
        name="project",
    )(index, cols, residual, residual_tan, *tokens, *weights)


def widened(mods, select):
    return pl.pallas_call(
        widen_kernel,
        out_shape=jax.ShapeDtypeStruct((mods.shape[1], 512), F32),
        in_specs=[VMEM, VMEM],
        out_specs=VMEM,
        compiler_params=pltpu.CompilerParams(vmem_limit_bytes=12 * 2**20),
        name="widen",
    )(mods, select)


def raise_up(index, spread, bias, tokens, weights, padded):
    rows, width = tokens[0].shape
    depth = rows * 16
    hidden = weights[0].shape[0]
    return pl.pallas_call(
        functools.partial(up_kernel, len(weights)),
        out_shape=jax.ShapeDtypeStruct((padded, width), BF16),
        in_specs=[SMEM, VMEM, VMEM] + [ANY] * (8 + len(weights)),
        out_specs=VMEM,
        scratch_shapes=[
            pltpu.VMEM((depth, width), BF16),
            pltpu.VMEM((2, 2 * rows, width), BF16),
            pltpu.VMEM((hidden, depth), BF16),
            pltpu.VMEM((hidden, width), F32),
            pltpu.SemaphoreType.DMA((16,)),
            pltpu.SemaphoreType.DMA((8,)),
        ],
        cost_estimate=cost(2 * hidden * depth * width, 2 * depth * (hidden + width)),
        compiler_params=pltpu.CompilerParams(vmem_limit_bytes=21 * 2**20),
        name="raise_up",
    )(index, spread, bias, *tokens, *weights)


def bring_down(index, act, weights):
    padded, width = act.shape
    rows = weights[0].shape[0] // 2
    depth = rows * 16
    pair = jax.ShapeDtypeStruct((2 * rows, width), BF16)
    return pl.pallas_call(
        functools.partial(down_kernel, len(weights)),
        out_shape=[pair] * 2 + [jax.ShapeDtypeStruct((4 * rows, width), BF16)] * 3,
        in_specs=[SMEM, VMEM] + [ANY] * len(weights),
        out_specs=[ANY] * 5,
        scratch_shapes=[
            pltpu.VMEM((depth, padded), BF16),
            pltpu.VMEM((depth, width), BF16),
            pltpu.SemaphoreType.DMA((8,)),
            pltpu.SemaphoreType.DMA((16,)),
        ],
        cost_estimate=cost(2 * padded * depth * width, 2 * depth * (padded + width)),
        compiler_params=pltpu.CompilerParams(vmem_limit_bytes=20 * 2**20),
        name="bring_down",
    )(index, act, *weights)


def add(*values):
    total = values[0].astype(F32)
    for value in values[1:]:
        total = total + value.astype(F32)
    return total


def scatter_sum(parts):
    far_a, far_b, plus, minus, own = parts
    half = far_a.shape[0]
    rows = half // 2
    from_a = send(far_a, 1, 1)
    from_b = send(far_b, 1, -1)
    plus = jnp.concatenate([add(plus[:half], from_a).astype(BF16), plus[half:]], axis=0)
    minus = jnp.concatenate([minus[:half], add(minus[half:], from_b).astype(BF16)], axis=0)
    total = add(own, send(plus, 1, 1), send(minus, 1, -1))
    low, high = total[:half], total[half:]
    near = [
        send(low[rows:].astype(BF16), 0, 1), send(high[rows:].astype(BF16), 0, -1), send(high[:rows].astype(BF16), 0, 2)
    ]
    return add(low[:rows], *near)


def index_table():
    row, col = lax.axis_index("row"), lax.axis_index("col")
    x, core = row // 2, row % 2
    z, y = col // 4, col % 4
    first, second = jnp.where(core == 0, y, z), jnp.where(core == 0, z, y)

    def column(one, two):
        return jnp.where(core == 0, two % 4 * 4 + one % 4, one % 4 * 4 + two % 4)

    shifts = jnp.array(SHIFTS, jnp.int32)
    plain = jnp.arange(4, dtype=jnp.int32)
    sources = column((first - shifts + 4)[None, :], (second - shifts + 4)[:, None]).reshape(16)
    targets = column((first + plain)[None, :], (second + plain)[:, None]).reshape(16)
    ring = (x - shifts + 4) % 4 * 2
    return jnp.concatenate([sources, targets, ring + core, ring + 1 - core]).astype(jnp.int32)


def body(
    attention,
    attention_tan,
    residual,
    residual_tan,
    modulation,
    modulation_tan,
    w_out,
    b_out,
    w_up,
    b_up,
    w_down,
    b_down,
):
    width = residual.shape[1]
    tokens = residual.shape[0] // CHUNKS
    index = index_table()
    col_offset = lax.axis_index("col") * width
    local = lax.dynamic_slice_in_dim(modulation, col_offset, width, 1)
    local_tan = lax.dynamic_slice_in_dim(modulation_tan, col_offset, width, 1)
    zero = jnp.zeros_like(b_out)
    cols = jnp.stack([local[0], local_tan[0], b_out, local[3], local_tan[3], b_down, zero, zero], axis=1)
    rows = jnp.stack([modulation[1], 1.0 + modulation[2], modulation_tan[1], modulation_tan[2]])
    high = lax.reduce_precision(rows, 8, 7)
    middle = lax.reduce_precision(rows - high, 8, 7)
    mods = jnp.concatenate([high, middle, rows - high - middle, jnp.zeros_like(rows)], axis=0).astype(BF16)
    select = jnp.concatenate([jnp.repeat(jnp.eye(4, dtype=BF16), 128, axis=1)] * 3 + [jnp.zeros((4, 512), BF16)], axis=0)
    up_bias = jnp.broadcast_to(b_up[:, None], (b_up.shape[0], 8))

    weights_out = gather_weight(w_out.T, True)

    def part(value, c):
        return value.T[:, c * tokens : (c + 1) * tokens]

    blocks = [jnp.concatenate([part(attention, c), part(attention_tan, c)], axis=1) for c in range(CHUNKS)]
    gathered, (index, cols) = gather_block(blocks[0], (index, cols))
    second, (mods, up_bias, turned) = gather_block(blocks[1], (mods, up_bias, turn(w_down)))
    gathered = [gathered, second]
    weights_up = gather_weight(w_up.T, True)
    weights_down = gather_weight(turned, True)
    streams = []
    for c in range(CHUNKS):
        streams.append(project(c, index, cols, residual.T, residual_tan.T, gathered[c], weights_out))
    gathered = [gather_block(streams[c]) for c in range(CHUNKS)]
    mods, late = lax.optimization_barrier((mods, streams[1]))
    spread = widened(mods, select)
    streams[1] = late
    outs = []
    for c in range(CHUNKS):
        act = raise_up(index, spread, up_bias, gathered[c], weights_up, turned.shape[1])
        parts = bring_down(index, act, weights_down)
        feeds = scatter_sum(parts)
        feed = feeds[:, :tokens] + cols[:, 5:6]
        feed_tan = feeds[:, tokens:]
        stream = streams[c].astype(F32)
        gate, gate_tan = cols[:, 3:4], cols[:, 4:5]
        out = (stream[:, :tokens] + gate * feed).astype(BF16)
        out_tan = (stream[:, tokens:] + gate_tan * feed + gate * feed_tan).astype(BF16)
        outs.append((out, out_tan))
    return tuple(jnp.concatenate([o[k] for o in outs], axis=1).T for k in range(2))


def solution(mesh):
    placed = (
        P("row", "col"),
        P("row", "col"),
        P("row", "col"),
        P("row", "col"),
        P(),
        P(),
        P("row", "col"),
        P("col"),
        P("row", "col"),
        P("col"),
        P("col", "row"),
        P("col"),
    )

    return jax.shard_map(
        body,
        mesh=mesh,
        in_specs=placed,
        out_specs=(P("row", "col"), P("row", "col")),
        check_vma=False,
    )
```
